32 devices in a mesh: walk: 4 (over y, x), pair: 8 (over z, core).
Axes of the slice: x: 2, y: 2, z: 4, core: 2. Of those that a mesh axis runs over, the one named last changes fastest.
Arguments:
- walkers: float32 [64, 64, 512], P(('walk', 'pair')), may hold values from -6 to 6
- inverse_intersection: float32 [64, 64, 64], P(('walk', 'pair')), may hold values from -0.75 to 0.75
- trial: bfloat16 [64, 512], P(None, 'walk'), may hold values from -0.095703125 to 0.095703125
- fields: float32 [64, 4096], P(('walk', 'pair')), may hold values from -6 to 6
- cholesky: bfloat16 [512, 512, 4096], P('pair', 'walk'), may hold values from -0.083984375 to 0.083984375
Outputs:
- advanced_walkers: float32 [64, 64, 512], P(('walk', 'pair'))
- log_importance: float32 [64], P(('walk', 'pair'))
The draws below stay inside these ranges and needn't reach their ends.
All inputs are finite; a program needn't handle non-finite values.
Results may differ from the reference program's by a relative error of at most 0.011.
Values may be sent and summed in bfloat16 or wider, within the bound.
No kernel may reach another device: no remote copies, remote signals or barrier semaphores. Data moves between devices by JAX's collectives and lax.ppermute only.
A program may use at most 128 MiB of HBM per device.

```python
import jax
import jax.numpy as jnp
from jax import lax

ORB = 512
OCC = 64
VECS = 4096
WALKERS = 64


def block_levels(key, dims, split, least, high):
    def one(position, blocks):
        heights = jax.random.uniform(jax.random.fold_in(jax.random.fold_in(key, 6), position), (blocks,), jnp.float32, least / len(split), high / len(split))
        return jnp.repeat(jnp.exp(heights), dims[position] // blocks).reshape((-1,) + (1,) * (len(dims) - position - 1))

    level = one(*split[0])
    for cut in split[1:]:
        level = level * one(*cut)
    return level


def bell_draw(rng, dims, deviation, most, cuts=(), kind=jnp.bfloat16):
    factor_of = block_levels(rng, dims, cuts, -0.22, 0.18) if cuts else 1.0
    array = jax.random.normal(rng, dims, jnp.float32) * deviation * factor_of
    return jnp.minimum(jnp.maximum(array, -most), most).astype(kind)


def setup_inputs(seed: int = 0) -> dict:
    arg_keys = jax.random.split(jax.random.key(seed), 6)
    return {
        "walkers": bell_draw(arg_keys[0], (WALKERS, OCC, ORB), 1.0, 6.0, ((0, 32),), jnp.float32),
        "inverse_intersection": bell_draw(arg_keys[1], (WALKERS, OCC, OCC), OCC ** -0.5, 0.75, ((0, 32),), jnp.float32),
        "trial": bell_draw(arg_keys[2], (OCC, ORB), 0.016, 0.095703125, ((1, 4),)),
        "fields": bell_draw(arg_keys[3], (WALKERS, VECS), 1.0, 6.0, ((0, 32),), jnp.float32),
        "cholesky": bell_draw(arg_keys[4], (ORB, ORB, VECS), (0.9 / VECS ** 0.5), 0.083984375, ((0, 8), (1, 4))),
    }


time_root = 0.1


def rounded(values):
    return lax.optimization_barrier(values.astype(jnp.bfloat16)).astype(jnp.float32)


def reference(walkers, inverse_intersection, trial, fields, cholesky):
    highest = lax.Precision.HIGHEST
    rotated = jnp.einsum("wji,wjp->wip", inverse_intersection, walkers, precision=highest)
    rotated = rounded(rotated)
    flat_slab = cholesky.reshape(ORB * ORB, VECS)
    trial_wide = trial.astype(jnp.float32)
    groups = WALKERS // 8

    def bias_block(rotated_block):
        greens = jnp.einsum("wip,iq->wpq", rotated_block, trial_wide, precision=highest)
        greens = greens.astype(jnp.bfloat16).reshape(8, ORB * ORB)
        return jnp.dot(greens, flat_slab, preferred_element_type=jnp.float32)

    force_bias = lax.map(bias_block, rotated.reshape(groups, 8, OCC, ORB)).reshape(WALKERS, VECS)
    bias_shift = -time_root * force_bias
    log_importance = jnp.sum(fields * bias_shift - 0.5 * bias_shift * bias_shift, axis=1)
    shifted = (fields - bias_shift).astype(jnp.bfloat16)

    def propagate(pair_args):
        walker_block, shifted_block = pair_args
        potential = jnp.dot(flat_slab, shifted_block.T, preferred_element_type=jnp.float32)
        potential = rounded(potential).T.reshape(8, ORB, ORB)
        series_term = walker_block
        summed = walker_block
        for degree in range(1, 7):
            series_term = jnp.einsum("kiq,kpq->kip", rounded(series_term), potential, precision=highest) * (-time_root / degree)
            summed = summed + series_term
        return summed

    advanced = lax.map(propagate, (walkers.reshape(groups, 8, OCC, ORB), shifted.reshape(groups, 8, VECS)))
    return advanced.reshape(WALKERS, OCC, ORB), log_importance
```

```python
import jax
import jax.numpy as jnp
from jax import lax
from jax.sharding import PartitionSpec as P

time_root = 0.1


def per_device(walkers, inverse_intersection, trial, fields, cholesky):
    highest = lax.Precision.HIGHEST
    pair_count = lax.axis_size("pair")
    walk_count = lax.axis_size("walk")
    local_walkers, occupied, orbitals = walkers.shape
    block_rows = cholesky.shape[0]
    block_cols = cholesky.shape[1]
    vectors = cholesky.shape[2]
    flat_slab = cholesky.reshape(block_rows * block_cols, vectors)
    split_walkers = walkers.reshape(local_walkers, occupied, pair_count, block_rows)
    rotated = jnp.einsum("wji,wjbr->wbir", inverse_intersection, split_walkers, precision=highest)
    rotated = rotated.astype(jnp.bfloat16).reshape(local_walkers, pair_count, occupied * block_rows)
    regrouped = lax.all_to_all(rotated, "pair", split_axis=1, concat_axis=0, tiled=True)
    shard_piece = lax.all_gather(regrouped, "walk", axis=0, tiled=True)
    rows_here = shard_piece.shape[0]
    rotated_piece = shard_piece.reshape(rows_here, occupied, block_rows)
    greens = jnp.einsum("wir,iq->wrq", rotated_piece, trial, preferred_element_type=jnp.float32)
    greens = greens.astype(jnp.bfloat16).reshape(rows_here, block_rows * block_cols)
    partial_bias = jnp.dot(greens, flat_slab, preferred_element_type=jnp.float32)
    rows_walk = rows_here // walk_count
    outgoing = partial_bias.astype(jnp.bfloat16).reshape(walk_count, rows_walk, vectors)
    incoming = lax.all_to_all(outgoing, "walk", split_axis=0, concat_axis=0, tiled=True)
    walk_sum = jnp.sum(incoming.astype(jnp.float32), axis=0)
    outgoing = walk_sum.astype(jnp.bfloat16).reshape(pair_count, local_walkers, vectors)
    incoming = lax.all_to_all(outgoing, "pair", split_axis=0, concat_axis=0, tiled=True)
    force_bias = jnp.sum(incoming.astype(jnp.float32), axis=0)
    own_shift = -time_root * force_bias
    log_importance = jnp.sum(fields * own_shift - 0.5 * own_shift * own_shift, axis=1)
    own_shifted = (fields - own_shift).astype(jnp.bfloat16)
    pair_shifted = lax.all_gather(own_shifted, "pair", axis=0, tiled=True)
    shifted = lax.all_gather(pair_shifted, "walk", axis=0, tiled=True)
    potential = lax.dot_general(
        shifted, flat_slab, (((1,), (1,)), ((), ())), preferred_element_type=jnp.float32
    )
    potential = potential.astype(jnp.bfloat16)
    blocks = potential.reshape(walk_count * pair_count, local_walkers, block_rows, block_cols)
    arrived = lax.all_to_all(blocks, ("walk", "pair"), split_axis=0, concat_axis=0, tiled=True)
    arrived = arrived.reshape(walk_count, pair_count, local_walkers, block_rows, block_cols)
    series_term = walkers
    summed = walkers
    for degree in range(1, 7):
        operand = series_term.astype(jnp.bfloat16).reshape(
            local_walkers, occupied, walk_count, block_cols
        )
        product = jnp.einsum(
            "kiac,abkrc->kibr", operand, arrived, preferred_element_type=jnp.float32
        )
        series_term = product.reshape(local_walkers, occupied, orbitals) * (-time_root / degree)
        summed = summed + series_term
    return (summed, log_importance)


def solution(mesh):
    in_specs = (
        P(("walk", "pair"), None, None),
        P(("walk", "pair"), None, None),
        P(None, "walk"),
        P(("walk", "pair"), None),
        P("pair", "walk", None),
    )
    out_specs = (P(("walk", "pair"), None, None), P(("walk", "pair")))
    return jax.shard_map(
        per_device, mesh=mesh, in_specs=in_specs, out_specs=out_specs, check_vma=False
    )
```

```python
import functools

import jax
import jax.numpy as jnp
from jax import lax
from jax.experimental import pallas as pl
from jax.experimental.pallas import tpu as pltpu
from jax.sharding import PartitionSpec as P

time_root = 0.1
lanes = 128
tile_rows = 512
row_group = 16
ring_slots = 2
ahead = 3
stream_slots = 4

mebi = 1 << 20
grant = 14 * mebi
highest = lax.Precision.HIGHEST
whole = pl.BlockSpec(memory_space=pltpu.VMEM)
anywhere = pl.BlockSpec(memory_space=pltpu.HBM)
scalar = pl.BlockSpec(memory_space=pltpu.SMEM)


def in_hbm(array):
    return pltpu.with_memory_space_constraint(array, pltpu.HBM)


def rotate_kernel(walkers_hbm, inverse_hbm, out_ref, walkers_ref, inverse_ref, sem):
    copies = [
        pltpu.make_async_copy(walkers_hbm, walkers_ref, sem.at[0]),
        pltpu.make_async_copy(inverse_hbm, inverse_ref, sem.at[1]),
    ]
    for copy in copies:
        copy.start()
    for copy in copies:
        copy.wait()
    count, occupied, orbitals = walkers_ref.shape
    half = out_ref.shape[1] // count
    pairs = orbitals // half // 2
    for w in range(count):
        turned = lax.dot_general(
            walkers_ref[w], inverse_ref[w], (((0,), (0,)), ((), ())),
            precision=highest, preferred_element_type=jnp.float32,
        )
        for b in range(pairs):
            low = turned[2 * b * half : (2 * b + 1) * half]
            high = turned[(2 * b + 1) * half : (2 * b + 2) * half]
            both = jnp.concatenate([low, high], axis=1).astype(jnp.bfloat16)
            for a in range(out_ref.shape[0] // pairs):
                out_ref[a * pairs + b, w * half : (w + 1) * half, :] = both


def rotate(walkers, inverse, walks, pairs):
    count, occupied, orbitals = walkers.shape
    half = orbitals // pairs // 2
    return pl.pallas_call(
        rotate_kernel,
        out_shape=jax.ShapeDtypeStruct(
            (walks * pairs, count * half, 2 * occupied), jnp.bfloat16
        ),
        in_specs=[anywhere, anywhere],
        out_specs=whole,
        scratch_shapes=[
            pltpu.VMEM(walkers.shape, jnp.float32),
            pltpu.VMEM(inverse.shape, jnp.float32),
            pltpu.SemaphoreType.DMA((2,)),
        ],
        compiler_params=pltpu.CompilerParams(vmem_limit_bytes=8 * mebi),
        name="rotate",
    )(in_hbm(walkers), in_hbm(inverse))


def bias_kernel(core_ref, rotated_ref, trial_ref, slab_ref, own_ref, sent_ref, kept_ref, wide, rows, greens, total, ring, kept_sem, ring_sem):
    vectors = total.shape[1]
    walkers_all = total.shape[0]
    half = rotated_ref.shape[0] // walkers_all
    occupied, columns = trial_ref.shape
    kept_tiles = kept_ref.shape[0] // tile_rows
    tiles = slab_ref.shape[0] // tile_rows
    blocks = vectors // lanes

    def kept_copy(t):
        span = pl.ds(pl.multiple_of(t * tile_rows, tile_rows), tile_rows)
        return pltpu.make_async_copy(slab_ref.at[span], kept_ref.at[span], kept_sem.at[t])

    def ring_copy(t):
        slot = lax.rem(t - kept_tiles, ring_slots)
        span = pl.ds(pl.multiple_of(t * tile_rows, tile_rows), tile_rows)
        return pltpu.make_async_copy(slab_ref.at[span], ring.at[slot], ring_sem.at[slot])

    for t in range(min(ahead, kept_tiles)):
        kept_copy(t).start()
    wide[: rotated_ref.shape[0], :] = rotated_ref[...].astype(jnp.float32)
    for r in range(half):
        rows[r * walkers_all : (r + 1) * walkers_all, :] = wide[
            pl.ds(r, walkers_all, stride=half), :
        ].astype(jnp.bfloat16)
    nothing = jnp.zeros((occupied, columns), jnp.bfloat16)
    trial = trial_ref[...]
    double = jnp.concatenate(
        [jnp.concatenate([trial, nothing], axis=1), jnp.concatenate([nothing, trial], axis=1)],
        axis=0,
    )
    step = 8
    for r0 in range(0, half, step):
        product = jnp.dot(
            rows[r0 * walkers_all : (r0 + step) * walkers_all, :], double,
            preferred_element_type=jnp.float32,
        ).astype(jnp.bfloat16)
        for r in range(step):
            piece = product[r * walkers_all : (r + 1) * walkers_all]
            first = (r0 + r) * columns
            second = (half + r0 + r) * columns
            greens[:, first : first + columns] = piece[:, :columns]
            greens[:, second : second + columns] = piece[:, columns:]
    total[...] = jnp.zeros_like(total)

    @pl.loop(0, kept_tiles)
    def _(t):
        start = pl.multiple_of(t * tile_rows, tile_rows)
        coming = t + ahead

        @pl.when(coming < kept_tiles)
        def _():
            kept_copy(coming).start()

        @pl.when((coming >= kept_tiles) & (coming < min(kept_tiles + ring_slots, tiles)))
        def _():
            ring_copy(coming).start()

        kept_copy(t).wait()
        total[...] += jnp.dot(
            greens[:, pl.ds(start, tile_rows)], kept_ref[pl.ds(start, tile_rows), :],
            preferred_element_type=jnp.float32,
        )

    @pl.loop(kept_tiles, tiles)
    def _(t):
        start = pl.multiple_of(t * tile_rows, tile_rows)
        slot = lax.rem(t - kept_tiles, ring_slots)
        ring_copy(t).wait()
        total[...] += jnp.dot(
            greens[:, pl.ds(start, tile_rows)], ring[slot],
            preferred_element_type=jnp.float32,
        )

        @pl.when(t + ring_slots < tiles)
        def _():
            ring_copy(t + ring_slots).start()

    for j in range(blocks):
        wide[j * walkers_all : (j + 1) * walkers_all, :] = total[:, j * lanes : (j + 1) * lanes]
    local_walkers = own_ref.shape[1] // blocks
    core = core_ref[0]
    for g in range(own_ref.shape[0]):
        for w in range(local_walkers):
            for ref, side in ((own_ref, core), (sent_ref, 1 - core)):
                row = (2 * g + side) * local_walkers + w
                ref[g, w * blocks : (w + 1) * blocks, :] = wide[
                    pl.ds(row, blocks, stride=walkers_all), :
                ].astype(jnp.bfloat16)


def bias_partial(core, local_walkers, rotated, trial, slab, walkers_all, kept_tiles):
    vectors = slab.shape[1]
    pairs = slab.shape[0]
    half_shape = (
        walkers_all // local_walkers // 2, local_walkers * vectors // lanes, lanes
    )
    height = max(rotated.shape[0], walkers_all * vectors // lanes)
    return pl.pallas_call(
        bias_kernel,
        out_shape=(
            jax.ShapeDtypeStruct(half_shape, jnp.bfloat16),
            jax.ShapeDtypeStruct(half_shape, jnp.bfloat16),
            pltpu.VMEM((kept_tiles * tile_rows, vectors), jnp.bfloat16),
        ),
        in_specs=[scalar, whole, whole, anywhere],
        out_specs=(whole, whole, whole),
        scratch_shapes=[
            pltpu.VMEM((height, lanes), jnp.float32),
            pltpu.VMEM(rotated.shape, jnp.bfloat16),
            pltpu.VMEM((walkers_all, pairs), jnp.bfloat16),
            pltpu.VMEM((walkers_all, vectors), jnp.float32),
            pltpu.VMEM((ring_slots, tile_rows, vectors), jnp.bfloat16),
            pltpu.SemaphoreType.DMA((kept_tiles,)),
            pltpu.SemaphoreType.DMA((ring_slots,)),
        ],
        compiler_params=pltpu.CompilerParams(vmem_limit_bytes=grant),
        cost_estimate=pl.CostEstimate(
            flops=2 * walkers_all * slab.size, bytes_accessed=2 * slab.size, transcendentals=0
        ),
        name="bias_partial",
    )(core, rotated, trial, slab)


def add_kernel(own_ref, other_ref, out_ref):
    added = own_ref[...].astype(jnp.float32) + other_ref[...].astype(jnp.float32)
    out_ref[...] = added.astype(jnp.bfloat16)


def add(own, other):
    return pl.pallas_call(
        add_kernel,
        out_shape=jax.ShapeDtypeStruct(own.shape, jnp.bfloat16),
        in_specs=[whole, whole],
        out_specs=whole,
        compiler_params=pltpu.CompilerParams(vmem_limit_bytes=4 * mebi),
        name="add",
    )(own, other)


def shift_kernel(in_ref, fields_ref, copies_ref, log_ref, turned):
    count, rows, _ = in_ref.shape
    local_walkers, vectors = fields_ref.shape
    blocks = vectors // lanes
    added = in_ref[0].astype(jnp.float32)
    for s in range(1, count):
        added = added + in_ref[s].astype(jnp.float32)
    bias_shift = -time_root * added
    for j in range(blocks):
        turned[j * local_walkers : (j + 1) * local_walkers, :] = fields_ref[
            :, j * lanes : (j + 1) * lanes
        ]
    for w in range(local_walkers):
        span = slice(w * blocks, (w + 1) * blocks)
        own = turned[pl.ds(w, blocks, stride=local_walkers), :]
        shift = bias_shift[span]
        shifted = (own - shift).astype(jnp.bfloat16)
        for s in range(copies_ref.shape[0]):
            copies_ref[s, span, :] = shifted
        score = jnp.sum(own * shift - 0.5 * shift * shift, axis=0, keepdims=True)
        log_ref[w : w + 1, :] = jnp.broadcast_to(
            jnp.sum(score, axis=1, keepdims=True), (1, lanes)
        )


def shift(incoming, fields):
    count, rows, _ = incoming.shape
    local_walkers = fields.shape[0]
    return pl.pallas_call(
        shift_kernel,
        out_shape=(
            jax.ShapeDtypeStruct((count, rows, lanes), jnp.bfloat16),
            jax.ShapeDtypeStruct((local_walkers, lanes), jnp.float32),
        ),
        in_specs=[whole, whole],
        out_specs=(whole, whole),
        scratch_shapes=[pltpu.VMEM((rows, lanes), jnp.float32)],
        compiler_params=pltpu.CompilerParams(vmem_limit_bytes=4 * mebi),
        name="shift",
    )(incoming, fields)


def potential_kernel(kept_tiles, core_ref, own_ref, other_ref, kept_ref, slab_ref, out_ref, wide, shifted, product, ring, ring_sem):
    half_rows = own_ref.shape[0]
    walkers_all, vectors = shifted.shape
    local_walkers = walkers_all // out_ref.shape[0]
    blocks = vectors // lanes
    tiles = slab_ref.shape[0] // tile_rows
    per_tile = tile_rows // lanes
    group = row_group // per_tile
    core = core_ref[0]

    def ring_copy(t):
        slot = (t - kept_tiles) % ring_slots
        span = pl.ds(t * tile_rows, tile_rows)
        return pltpu.make_async_copy(slab_ref.at[span], ring.at[slot], ring_sem.at[slot])

    for t in range(kept_tiles, min(kept_tiles + ring_slots, tiles)):
        ring_copy(t).start()
    wide[:half_rows, :] = own_ref[...].astype(jnp.float32)
    wide[half_rows:, :] = other_ref[...].astype(jnp.float32)
    for j in range(blocks):
        shifted[:, j * lanes : (j + 1) * lanes] = wide[
            pl.ds(j, walkers_all, stride=blocks), :
        ].astype(jnp.bfloat16)
    for t in range(tiles):
        if t < kept_tiles:
            tile = kept_ref[t * tile_rows : (t + 1) * tile_rows, :]
        else:
            ring_copy(t).wait()
            tile = ring[(t - kept_tiles) % ring_slots]
        values = lax.dot_general(
            shifted[...], tile, (((1,), (1,)), ((), ())), preferred_element_type=jnp.float32
        )
        if t >= kept_tiles and t + ring_slots < tiles:
            ring_copy(t + ring_slots).start()
        place = t % group * per_tile
        for r in range(per_tile):
            product[(place + r) * walkers_all : (place + r + 1) * walkers_all, :] = values[
                :, r * lanes : (r + 1) * lanes
            ]
        if t % group == group - 1:
            base = t // group * row_group
            for m in range(walkers_all):
                side, rest = divmod(m, walkers_all // 2)
                g, w = divmod(rest, local_walkers)
                owner = 2 * g + (core if side == 0 else 1 - core)
                out_ref[owner, w, base : base + row_group, :] = product[
                    pl.ds(m, row_group, stride=walkers_all), :
                ].astype(jnp.bfloat16)


def potential(core, local_walkers, own, other, kept, slab, kept_tiles):
    vectors = slab.shape[1]
    walkers_all = 2 * own.shape[0] * lanes // vectors
    rows = slab.shape[0] // lanes
    return pl.pallas_call(
        functools.partial(potential_kernel, kept_tiles),
        out_shape=jax.ShapeDtypeStruct(
            (walkers_all // local_walkers, local_walkers, rows, lanes), jnp.bfloat16
        ),
        in_specs=[scalar, whole, whole, whole, anywhere],
        out_specs=whole,
        scratch_shapes=[
            pltpu.VMEM((2 * own.shape[0], lanes), jnp.float32),
            pltpu.VMEM((walkers_all, vectors), jnp.bfloat16),
            pltpu.VMEM((row_group * walkers_all, lanes), jnp.float32),
            pltpu.VMEM((ring_slots, tile_rows, vectors), jnp.bfloat16),
            pltpu.SemaphoreType.DMA((ring_slots,)),
        ],
        compiler_params=pltpu.CompilerParams(vmem_limit_bytes=grant),
        cost_estimate=pl.CostEstimate(
            flops=2 * walkers_all * slab.size, bytes_accessed=2 * slab.size, transcendentals=0
        ),
        name="potential",
    )(core, own, other, pltpu.with_memory_space_constraint(kept, pltpu.VMEM), slab)


def series_kernel(walk_count, walkers_ref, *refs):
    pieces, out_ref, matrix = refs[:-2], refs[-2], refs[-1]
    local_walkers, occupied, orbitals = walkers_ref.shape
    pair_count = pieces[0].shape[0] // walk_count
    block_rows = orbitals // pair_count
    for w in range(local_walkers):
        at = 0
        for piece in pieces:
            rows = piece.shape[2]
            for a in range(walk_count):
                for b in range(pair_count):
                    top = b * block_rows + at
                    matrix[w, top : top + rows, a * lanes : (a + 1) * lanes] = piece[
                        a * pair_count + b, w
                    ]
            at += rows
    terms = [walkers_ref[w] for w in range(local_walkers)]
    sums = list(terms)
    for degree in range(1, 7):
        for w in range(local_walkers):
            terms[w] = lax.dot_general(
                terms[w].astype(jnp.bfloat16), matrix[w], (((1,), (1,)), ((), ())),
                preferred_element_type=jnp.float32,
            ) * (-time_root / degree)
            sums[w] = sums[w] + terms[w]
    for w in range(local_walkers):
        out_ref[w] = sums[w]


def series(walkers, pieces, walk_count):
    local_walkers, occupied, orbitals = walkers.shape
    return pl.pallas_call(
        functools.partial(series_kernel, walk_count),
        out_shape=jax.ShapeDtypeStruct(walkers.shape, jnp.float32),
        in_specs=[whole] * (1 + len(pieces)),
        out_specs=whole,
        scratch_shapes=[pltpu.VMEM((local_walkers, orbitals, orbitals), jnp.bfloat16)],
        compiler_params=pltpu.CompilerParams(vmem_limit_bytes=16 * mebi),
        name="series",
    )(walkers, *pieces)


kept_share = 0.6875


def fast(walkers, inverse_intersection, trial, fields, cholesky):
    pair_count = lax.axis_size("pair")
    walk_count = lax.axis_size("walk")
    device_count = walk_count * pair_count
    local_walkers, occupied, orbitals = walkers.shape
    walkers_all = local_walkers * device_count
    vectors = cholesky.shape[2]
    blocks = vectors // lanes
    slab = cholesky.reshape(-1, vectors)
    tiles = slab.shape[0] // tile_rows
    kept_tiles = int(tiles * kept_share)
    everyone = ("walk", "pair")
    exchange = functools.partial(
        lax.all_to_all, axis_name=everyone, split_axis=0, concat_axis=0, tiled=True
    )
    rotated = rotate(walkers, inverse_intersection, walk_count, pair_count)
    pieces = exchange(rotated).reshape(-1, 2 * occupied)
    place = lax.axis_index("pair")
    core = lax.rem(place, 2).reshape(1)
    swap = [(i, i ^ 1) for i in range(pair_count)]
    alike = [list(range(c, device_count, 2)) for c in range(2)]
    own, sent, kept = bias_partial(
        core, local_walkers, pieces, trial, slab, walkers_all, kept_tiles
    )
    incoming = exchange(add(own, lax.ppermute(sent, "pair", swap)), axis_index_groups=alike)
    copies, log_rows = shift(incoming, fields)
    own = exchange(copies, axis_index_groups=alike).reshape(-1, lanes)
    other = lax.ppermute(own, "pair", swap)
    arrived = [exchange(potential(core, local_walkers, own, other, kept, slab, kept_tiles))]
    return (series(walkers, arrived, walk_count), log_rows[:, 0])


def plain(walkers, inverse_intersection, trial, fields, cholesky):
    pair_count = lax.axis_size("pair")
    walk_count = lax.axis_size("walk")
    local_walkers, occupied, orbitals = walkers.shape
    block_rows = cholesky.shape[0]
    block_cols = cholesky.shape[1]
    vectors = cholesky.shape[2]
    flat_slab = cholesky.reshape(block_rows * block_cols, vectors)
    split_walkers = walkers.reshape(local_walkers, occupied, pair_count, block_rows)
    rotated = jnp.einsum("wji,wjbr->wbir", inverse_intersection, split_walkers, precision=highest)
    rotated = rotated.astype(jnp.bfloat16).reshape(local_walkers, pair_count, occupied * block_rows)
    regrouped = lax.all_to_all(rotated, "pair", split_axis=1, concat_axis=0, tiled=True)
    shard_piece = lax.all_gather(regrouped, "walk", axis=0, tiled=True)
    rows_here = shard_piece.shape[0]
    rotated_piece = shard_piece.reshape(rows_here, occupied, block_rows)
    greens = jnp.einsum("wir,iq->wrq", rotated_piece, trial, preferred_element_type=jnp.float32)
    greens = greens.astype(jnp.bfloat16).reshape(rows_here, block_rows * block_cols)
    partial_bias = jnp.dot(greens, flat_slab, preferred_element_type=jnp.float32)
    rows_walk = rows_here // walk_count
    outgoing = partial_bias.astype(jnp.bfloat16).reshape(walk_count, rows_walk, vectors)
    incoming = lax.all_to_all(outgoing, "walk", split_axis=0, concat_axis=0, tiled=True)
    walk_sum = jnp.sum(incoming.astype(jnp.float32), axis=0)
    outgoing = walk_sum.astype(jnp.bfloat16).reshape(pair_count, local_walkers, vectors)
    incoming = lax.all_to_all(outgoing, "pair", split_axis=0, concat_axis=0, tiled=True)
    force_bias = jnp.sum(incoming.astype(jnp.float32), axis=0)
    own_shift = -time_root * force_bias
    log_importance = jnp.sum(fields * own_shift - 0.5 * own_shift * own_shift, axis=1)
    own_shifted = (fields - own_shift).astype(jnp.bfloat16)
    pair_shifted = lax.all_gather(own_shifted, "pair", axis=0, tiled=True)
    shifted = lax.all_gather(pair_shifted, "walk", axis=0, tiled=True)
    potential = lax.dot_general(
        shifted, flat_slab, (((1,), (1,)), ((), ())), preferred_element_type=jnp.float32
    )
    potential = potential.astype(jnp.bfloat16)
    blocks = potential.reshape(walk_count * pair_count, local_walkers, block_rows, block_cols)
    arrived = lax.all_to_all(blocks, ("walk", "pair"), split_axis=0, concat_axis=0, tiled=True)
    arrived = arrived.reshape(walk_count, pair_count, local_walkers, block_rows, block_cols)
    series_term = walkers
    summed = walkers
    for degree in range(1, 7):
        operand = series_term.astype(jnp.bfloat16).reshape(
            local_walkers, occupied, walk_count, block_cols
        )
        product = jnp.einsum(
            "kiac,abkrc->kibr", operand, arrived, preferred_element_type=jnp.float32
        )
        series_term = product.reshape(local_walkers, occupied, orbitals) * (-time_root / degree)
        summed = summed + series_term
    return (summed, log_importance)

def per_device(walkers, inverse_intersection, trial, fields, cholesky):
    block_rows, block_cols, vectors = cholesky.shape
    fits = (
        block_cols == lanes
        and vectors % lanes == 0
        and 2 * walkers.shape[1] == lanes
        and block_rows % 32 == 0
        and lax.axis_size("pair") % 2 == 0
    )
    step = fast if fits else plain
    return step(walkers, inverse_intersection, trial, fields, cholesky)


def solution(mesh):
    in_specs = (
        P(("walk", "pair"), None, None),
        P(("walk", "pair"), None, None),
        P(None, "walk"),
        P(("walk", "pair"), None),
        P("pair", "walk", None),
    )
    out_specs = (P(("walk", "pair"), None, None), P(("walk", "pair")))
    return jax.shard_map(
        per_device, mesh=mesh, in_specs=in_specs, out_specs=out_specs, check_vma=False
    )
```

```python
import functools

import jax
import jax.numpy as jnp
from jax import lax
from jax.experimental import pallas as pl
from jax.experimental.pallas import tpu as pltpu
from jax.sharding import PartitionSpec as P

time_root = 0.1
lanes = 128
tile_rows = 512
ring_slots = 2
ahead = 6
period = 4
early_share = 0.34

mebi = 1 << 20
grant = 13 * mebi
highest = lax.Precision.HIGHEST
whole = pl.BlockSpec(memory_space=pltpu.VMEM)
anywhere = pl.BlockSpec(memory_space=pltpu.HBM)
scalar = pl.BlockSpec(memory_space=pltpu.SMEM)


def in_vmem(array):
    return pltpu.with_memory_space_constraint(array, pltpu.VMEM)


def in_hbm(array):
    return pltpu.with_memory_space_constraint(array, pltpu.HBM)


def rotate_kernel(walkers_hbm, inverse_hbm, out_ref, walkers_ref, inverse_ref, sem):
    copies = [
        pltpu.make_async_copy(walkers_hbm, walkers_ref, sem.at[0]),
        pltpu.make_async_copy(inverse_hbm, inverse_ref, sem.at[1]),
    ]
    for copy in copies:
        copy.start()
    for copy in copies:
        copy.wait()
    count, _, orbitals = walkers_ref.shape
    half = out_ref.shape[1] // count
    pairs = orbitals // half // 2
    for w in range(count):
        turned = lax.dot_general(
            walkers_ref[w], inverse_ref[w], (((0,), (0,)), ((), ())),
            precision=highest, preferred_element_type=jnp.float32,
        )
        for b in range(pairs):
            low = turned[2 * b * half : (2 * b + 1) * half]
            high = turned[(2 * b + 1) * half : (2 * b + 2) * half]
            both = jnp.concatenate([low, high], axis=1).astype(jnp.bfloat16)
            for a in range(out_ref.shape[0] // pairs):
                out_ref[a * pairs + b, w * half : (w + 1) * half, :] = both


def rotate(walkers, inverse, walks, pairs):
    count, occupied, orbitals = walkers.shape
    half = orbitals // pairs // 2
    return pl.pallas_call(
        rotate_kernel,
        out_shape=jax.ShapeDtypeStruct(
            (walks * pairs, count * half, 2 * occupied), jnp.bfloat16
        ),
        in_specs=[anywhere, anywhere],
        out_specs=whole,
        scratch_shapes=[
            pltpu.VMEM(walkers.shape, jnp.float32),
            pltpu.VMEM(inverse.shape, jnp.float32),
            pltpu.SemaphoreType.DMA((2,)),
        ],
        compiler_params=pltpu.CompilerParams(vmem_limit_bytes=8 * mebi),
        name="rotate",
    )(in_hbm(walkers), in_hbm(inverse))


def pitch_of(rows):
    return rows + 8


def tile_access(slab_ref, kept_ref, ring, kept_sem, ring_sem):
    def view(group, i):
        if i == period - 1:
            return ring.at[group % ring_slots]
        start = (group * (period - 1) + i) * tile_rows
        return kept_ref.at[pl.ds(start, tile_rows)]

    def fetch(group, i):
        span = pl.ds((group * period + i) * tile_rows, tile_rows)
        if i == period - 1:
            sem = ring_sem.at[group % ring_slots]
        else:
            sem = kept_sem.at[group * (period - 1) + i]
        return pltpu.make_async_copy(slab_ref.at[span], view(group, i), sem)

    return fetch, view


def load_kernel(early, after_ref, slab_ref, kept_ref, sem):
    fetch, _ = tile_access(slab_ref, kept_ref, None, sem, None)
    chosen = [fetch(t // period, t % period) for t in early]
    for copy in chosen:
        copy.start()
    for copy in chosen:
        copy.wait()


def bias_kernel(count, early, core_ref, place_ref, *refs):
    parts, refs = refs[:count], refs[count:]
    trial_ref, _, slab_ref, own_ref, sent_ref, kept_ref, wide, rows, greens, total, ring, kept_sem, ring_sem = refs
    vectors = total.shape[1]
    walkers_all = total.shape[0]
    group_walkers = walkers_all // count
    half = parts[0].shape[0] // group_walkers
    occupied, columns = trial_ref.shape
    tiles = slab_ref.shape[0] // tile_rows
    blocks = vectors // lanes
    fetch, view = tile_access(slab_ref, kept_ref, ring, kept_sem, ring_sem)

    for t in range(min(ahead, tiles)):
        if t not in early:
            fetch(t // period, t % period).start()
    pitch = pitch_of(half)
    for k, part in enumerate(parts):
        top = (place_ref[0] ^ k) * (group_walkers * pitch)
        for w in range(group_walkers):
            row = pl.multiple_of(top + w * pitch, 8)
            wide[pl.ds(row, half), :] = part[w * half : (w + 1) * half, :].astype(jnp.float32)
    for r in range(half):
        rows[r * walkers_all : (r + 1) * walkers_all, :] = wide[
            pl.ds(r, walkers_all, stride=pitch), :
        ].astype(jnp.bfloat16)
    nothing = jnp.zeros((occupied, columns), jnp.bfloat16)
    trial = trial_ref[...]
    double = jnp.concatenate(
        [jnp.concatenate([trial, nothing], axis=1), jnp.concatenate([nothing, trial], axis=1)],
        axis=0,
    )
    step = 8
    for r0 in range(0, half, step):
        product = jnp.dot(
            rows[r0 * walkers_all : (r0 + step) * walkers_all, :], double,
            preferred_element_type=jnp.float32,
        ).astype(jnp.bfloat16)
        for r in range(step):
            piece = product[r * walkers_all : (r + 1) * walkers_all]
            first = (r0 + r) * columns
            second = (half + r0 + r) * columns
            greens[:, first : first + columns] = piece[:, :columns]
            greens[:, second : second + columns] = piece[:, columns:]
    total[...] = jnp.zeros_like(total)

    for group in range(tiles // period):
        for i in range(period):
            t = group * period + i
            if t + ahead < tiles and t + ahead not in early:
                fetch((t + ahead) // period, (t + ahead) % period).start()
            if t not in early:
                fetch(group, i).wait()
            total[...] += jnp.dot(
                greens[:, t * tile_rows : (t + 1) * tile_rows], view(group, i)[...],
                preferred_element_type=jnp.float32,
            )

    pitch = pitch_of(walkers_all)
    for j in range(blocks):
        wide[j * pitch : j * pitch + walkers_all, :] = total[:, j * lanes : (j + 1) * lanes]
    local_walkers = own_ref.shape[1] // blocks
    core = core_ref[0]
    for g in range(own_ref.shape[0]):
        for w in range(local_walkers):
            for ref, side in ((own_ref, core), (sent_ref, 1 - core)):
                row = (2 * g + side) * local_walkers + w
                ref[g, w * blocks : (w + 1) * blocks, :] = wide[
                    pl.ds(row, blocks, stride=pitch), :
                ].astype(jnp.bfloat16)


def tiles_of(slab):
    return slab.shape[0] // tile_rows


def early_tiles(slab):
    kept = [t for t in range(tiles_of(slab)) if t % period < period - 1]
    return tuple(kept[: int(len(kept) * early_share)])


def load(after, slab):
    vectors = slab.shape[1]
    kept_tiles = tiles_of(slab) // period * (period - 1)
    early = early_tiles(slab)
    return pl.pallas_call(
        functools.partial(load_kernel, early),
        out_shape=pltpu.VMEM((kept_tiles * tile_rows, vectors), jnp.bfloat16),
        in_specs=[pl.BlockSpec(memory_space=pl.ANY), anywhere],
        out_specs=whole,
        scratch_shapes=[pltpu.SemaphoreType.DMA((kept_tiles,))],
        compiler_params=pltpu.CompilerParams(vmem_limit_bytes=grant),
        cost_estimate=pl.CostEstimate(
            flops=0,
            bytes_accessed=2 * len(early) * tile_rows * vectors,
            transcendentals=0,
        ),
        name="load",
    )(after, slab)


def bias_partial(core, place, local_walkers, parts, trial, kept, slab, walkers_all):
    vectors = slab.shape[1]
    pairs = slab.shape[0]
    count = len(parts)
    half = parts[0].shape[0] * count // walkers_all
    half_shape = (
        walkers_all // local_walkers // 2, local_walkers * vectors // lanes, lanes
    )
    height = max(walkers_all * pitch_of(half), vectors // lanes * pitch_of(walkers_all))
    return pl.pallas_call(
        functools.partial(bias_kernel, count, early_tiles(slab)),
        out_shape=(
            jax.ShapeDtypeStruct(half_shape, jnp.bfloat16),
            jax.ShapeDtypeStruct(half_shape, jnp.bfloat16),
            pltpu.VMEM(kept.shape, jnp.bfloat16),
        ),
        in_specs=[scalar] * 2 + [whole] * (count + 2) + [anywhere],
        out_specs=(whole, whole, whole),
        input_output_aliases={count + 3: 2},
        scratch_shapes=[
            pltpu.VMEM((height, lanes), jnp.float32),
            pltpu.VMEM((walkers_all * half, lanes), jnp.bfloat16),
            pltpu.VMEM((walkers_all, pairs), jnp.bfloat16),
            pltpu.VMEM((walkers_all, vectors), jnp.float32),
            pltpu.VMEM((ring_slots, tile_rows, vectors), jnp.bfloat16),
            pltpu.SemaphoreType.DMA((tiles_of(slab),)),
            pltpu.SemaphoreType.DMA((ring_slots,)),
        ],
        compiler_params=pltpu.CompilerParams(vmem_limit_bytes=grant),
        cost_estimate=pl.CostEstimate(
            flops=2 * walkers_all * slab.size, bytes_accessed=2 * slab.size, transcendentals=0
        ),
        name="bias_partial",
    )(core, place, *[in_vmem(part) for part in parts], trial, pltpu.with_memory_space_constraint(kept, pltpu.VMEM), slab)


def add_kernel(own_ref, other_ref, out_ref):
    added = own_ref[...].astype(jnp.float32) + other_ref[...].astype(jnp.float32)
    out_ref[...] = added.astype(jnp.bfloat16)


def add(own, other):
    return pl.pallas_call(
        add_kernel,
        out_shape=jax.ShapeDtypeStruct(own.shape, jnp.bfloat16),
        in_specs=[whole, whole],
        out_specs=whole,
        compiler_params=pltpu.CompilerParams(vmem_limit_bytes=4 * mebi),
        name="add",
    )(own, other)


def shift_kernel(in_ref, fields_ref, copies_ref, log_ref, turned):
    count, _, _ = in_ref.shape
    local_walkers, vectors = fields_ref.shape
    blocks = vectors // lanes
    added = in_ref[0].astype(jnp.float32)
    for s in range(1, count):
        added = added + in_ref[s].astype(jnp.float32)
    bias_shift = -time_root * added
    for j in range(blocks):
        turned[j * local_walkers : (j + 1) * local_walkers, :] = fields_ref[
            :, j * lanes : (j + 1) * lanes
        ]
    for w in range(local_walkers):
        span = slice(w * blocks, (w + 1) * blocks)
        own = turned[pl.ds(w, blocks, stride=local_walkers), :]
        shift = bias_shift[span]
        shifted = (own - shift).astype(jnp.bfloat16)
        for s in range(copies_ref.shape[0]):
            copies_ref[s, span, :] = shifted
        score = jnp.sum(own * shift - 0.5 * shift * shift, axis=0, keepdims=True)
        log_ref[w : w + 1, :] = jnp.broadcast_to(
            jnp.sum(score, axis=1, keepdims=True), (1, lanes)
        )


def shift(incoming, fields):
    count, rows, _ = incoming.shape
    local_walkers = fields.shape[0]
    return pl.pallas_call(
        shift_kernel,
        out_shape=(
            jax.ShapeDtypeStruct((count, rows, lanes), jnp.bfloat16),
            jax.ShapeDtypeStruct((local_walkers, lanes), jnp.float32),
        ),
        in_specs=[whole, whole],
        out_specs=(whole, whole),
        scratch_shapes=[pltpu.VMEM((rows, lanes), jnp.float32)],
        compiler_params=pltpu.CompilerParams(vmem_limit_bytes=4 * mebi),
        name="shift",
    )(incoming, fields)


def potential_kernel(core_ref, own_ref, other_ref, kept_ref, slab_ref, out_ref, wide, shifted, product, ring, ring_sem):
    half_rows = own_ref.shape[0]
    walkers_all, vectors = shifted.shape
    local_walkers = walkers_all // out_ref.shape[0]
    blocks = vectors // lanes
    groups = slab_ref.shape[0] // tile_rows // period
    per_tile = tile_rows // lanes
    group_rows = period * per_tile
    core = core_ref[0]
    fetch, view = tile_access(slab_ref, kept_ref, ring, None, ring_sem)

    for group in range(min(ring_slots, groups)):
        fetch(group, period - 1).start()
    pitch = pitch_of(blocks)
    for m in range(walkers_all):
        ref, row = (own_ref, m * blocks) if m * blocks < half_rows else (
            other_ref, m * blocks - half_rows
        )
        wide[m * pitch : m * pitch + blocks, :] = ref[row : row + blocks, :].astype(jnp.float32)
    for j in range(blocks):
        shifted[:, j * lanes : (j + 1) * lanes] = wide[
            pl.ds(j, walkers_all, stride=pitch), :
        ].astype(jnp.bfloat16)
    pitch = pitch_of(walkers_all)
    for group in range(groups):
        half = group % 2
        for i in range(period):
            if i == period - 1:
                fetch(group, i).wait()
            values = lax.dot_general(
                view(group, i)[...], shifted[...], (((1,), (1,)), ((), ())),
                preferred_element_type=jnp.float32,
            ).T
            for r in range(per_tile):
                row = (i * per_tile + r) * pitch
                product[half, row : row + walkers_all, :] = values[:, r * lanes : (r + 1) * lanes]
        if group + ring_slots < groups:
            fetch(group + ring_slots, period - 1).start()
        base = group * group_rows
        for m in range(walkers_all):
            side, rest = divmod(m, walkers_all // 2)
            g, w = divmod(rest, local_walkers)
            owner = 2 * g + (core if side == 0 else 1 - core)
            out_ref[owner, w, base : base + group_rows, :] = product[
                half, pl.ds(m, group_rows, stride=pitch), :
            ].astype(jnp.bfloat16)


def potential(core, local_walkers, own, other, kept, slab):
    vectors = slab.shape[1]
    walkers_all = 2 * own.shape[0] * lanes // vectors
    rows = slab.shape[0] // lanes
    return pl.pallas_call(
        potential_kernel,
        out_shape=jax.ShapeDtypeStruct(
            (walkers_all // local_walkers, local_walkers, rows, lanes), jnp.bfloat16
        ),
        in_specs=[scalar, whole, whole, whole, anywhere],
        out_specs=whole,
        scratch_shapes=[
            pltpu.VMEM((walkers_all * pitch_of(vectors // lanes), lanes), jnp.float32),
            pltpu.VMEM((walkers_all, vectors), jnp.bfloat16),
            pltpu.VMEM((2, tile_rows // lanes * period * pitch_of(walkers_all), lanes), jnp.float32),
            pltpu.VMEM((ring_slots, tile_rows, vectors), jnp.bfloat16),
            pltpu.SemaphoreType.DMA((ring_slots,)),
        ],
        compiler_params=pltpu.CompilerParams(vmem_limit_bytes=grant),
        cost_estimate=pl.CostEstimate(
            flops=2 * walkers_all * slab.size, bytes_accessed=2 * slab.size, transcendentals=0
        ),
        name="potential",
    )(core, own, other, pltpu.with_memory_space_constraint(kept, pltpu.VMEM), slab)


def series_kernel(walk_count, walkers_ref, *refs):
    pieces, out_ref, matrix = refs[:-2], refs[-2], refs[-1]
    local_walkers, _, orbitals = walkers_ref.shape
    pair_count = pieces[0].shape[0] // walk_count
    block_rows = orbitals // pair_count
    for w in range(local_walkers):
        at = 0
        for piece in pieces:
            rows = piece.shape[2]
            for a in range(walk_count):
                for b in range(pair_count):
                    top = b * block_rows + at
                    matrix[w, top : top + rows, a * lanes : (a + 1) * lanes] = piece[
                        a * pair_count + b, w
                    ]
            at += rows
    terms = [walkers_ref[w] for w in range(local_walkers)]
    sums = list(terms)
    for degree in range(1, 7):
        for w in range(local_walkers):
            terms[w] = lax.dot_general(
                terms[w].astype(jnp.bfloat16), matrix[w], (((1,), (1,)), ((), ())),
                preferred_element_type=jnp.float32,
            ) * (-time_root / degree)
            sums[w] = sums[w] + terms[w]
    for w in range(local_walkers):
        out_ref[w] = sums[w]


def series(walkers, pieces, walk_count):
    local_walkers, _, orbitals = walkers.shape
    return pl.pallas_call(
        functools.partial(series_kernel, walk_count),
        out_shape=jax.ShapeDtypeStruct(walkers.shape, jnp.float32),
        in_specs=[whole] * (1 + len(pieces)),
        out_specs=whole,
        scratch_shapes=[pltpu.VMEM((local_walkers, orbitals, orbitals), jnp.bfloat16)],
        compiler_params=pltpu.CompilerParams(vmem_limit_bytes=16 * mebi),
        name="series",
    )(walkers, *pieces)


def fast(walkers, inverse_intersection, trial, fields, cholesky):
    pair_count = lax.axis_size("pair")
    walk_count = lax.axis_size("walk")
    device_count = walk_count * pair_count
    local_walkers, occupied, _ = walkers.shape
    walkers_all = local_walkers * device_count
    vectors = cholesky.shape[2]
    slab = cholesky.reshape(-1, vectors)
    everyone = ("walk", "pair")
    exchange = functools.partial(
        lax.all_to_all, axis_name=everyone, split_axis=0, concat_axis=0, tiled=True
    )
    rotated = rotate(walkers, inverse_intersection, 1, pair_count)
    regrouped = lax.all_to_all(rotated, "pair", split_axis=0, concat_axis=0, tiled=True)
    regrouped = regrouped.reshape(-1, 2 * occupied)
    parts = [regrouped]
    for k in range(1, walk_count):
        route = [(i, i ^ k) for i in range(walk_count)]
        parts.append(lax.ppermute(regrouped, "walk", route))
    kept = load(regrouped, slab)
    core = lax.rem(lax.axis_index("pair"), 2).reshape(1)
    place = lax.axis_index("walk").reshape(1)
    swap = [(i, i ^ 1) for i in range(pair_count)]
    alike = [list(range(c, device_count, 2)) for c in range(2)]
    own, sent, kept = bias_partial(
        core, place, local_walkers, parts, trial, kept, slab, walkers_all
    )
    incoming = exchange(add(own, lax.ppermute(sent, "pair", swap)), axis_index_groups=alike)
    copies, log_rows = shift(incoming, fields)
    own = exchange(copies, axis_index_groups=alike).reshape(-1, lanes)
    other = lax.ppermute(own, "pair", swap)
    arrived = [exchange(potential(core, local_walkers, own, other, kept, slab))]
    return (series(walkers, arrived, walk_count), log_rows[:, 0])


def plain(walkers, inverse_intersection, trial, fields, cholesky):
    pair_count = lax.axis_size("pair")
    walk_count = lax.axis_size("walk")
    local_walkers, occupied, orbitals = walkers.shape
    block_rows = cholesky.shape[0]
    block_cols = cholesky.shape[1]
    vectors = cholesky.shape[2]
    flat_slab = cholesky.reshape(block_rows * block_cols, vectors)
    split_walkers = walkers.reshape(local_walkers, occupied, pair_count, block_rows)
    rotated = jnp.einsum("wji,wjbr->wbir", inverse_intersection, split_walkers, precision=highest)
    rotated = rotated.astype(jnp.bfloat16).reshape(local_walkers, pair_count, occupied * block_rows)
    regrouped = lax.all_to_all(rotated, "pair", split_axis=1, concat_axis=0, tiled=True)
    shard_piece = lax.all_gather(regrouped, "walk", axis=0, tiled=True)
    rows_here = shard_piece.shape[0]
    rotated_piece = shard_piece.reshape(rows_here, occupied, block_rows)
    greens = jnp.einsum("wir,iq->wrq", rotated_piece, trial, preferred_element_type=jnp.float32)
    greens = greens.astype(jnp.bfloat16).reshape(rows_here, block_rows * block_cols)
    partial_bias = jnp.dot(greens, flat_slab, preferred_element_type=jnp.float32)
    rows_walk = rows_here // walk_count
    outgoing = partial_bias.astype(jnp.bfloat16).reshape(walk_count, rows_walk, vectors)
    incoming = lax.all_to_all(outgoing, "walk", split_axis=0, concat_axis=0, tiled=True)
    walk_sum = jnp.sum(incoming.astype(jnp.float32), axis=0)
    outgoing = walk_sum.astype(jnp.bfloat16).reshape(pair_count, local_walkers, vectors)
    incoming = lax.all_to_all(outgoing, "pair", split_axis=0, concat_axis=0, tiled=True)
    force_bias = jnp.sum(incoming.astype(jnp.float32), axis=0)
    own_shift = -time_root * force_bias
    log_importance = jnp.sum(fields * own_shift - 0.5 * own_shift * own_shift, axis=1)
    own_shifted = (fields - own_shift).astype(jnp.bfloat16)
    pair_shifted = lax.all_gather(own_shifted, "pair", axis=0, tiled=True)
    shifted = lax.all_gather(pair_shifted, "walk", axis=0, tiled=True)
    potential = lax.dot_general(
        shifted, flat_slab, (((1,), (1,)), ((), ())), preferred_element_type=jnp.float32
    )
    potential = potential.astype(jnp.bfloat16)
    blocks = potential.reshape(walk_count * pair_count, local_walkers, block_rows, block_cols)
    arrived = lax.all_to_all(blocks, ("walk", "pair"), split_axis=0, concat_axis=0, tiled=True)
    arrived = arrived.reshape(walk_count, pair_count, local_walkers, block_rows, block_cols)
    series_term = walkers
    summed = walkers
    for degree in range(1, 7):
        operand = series_term.astype(jnp.bfloat16).reshape(
            local_walkers, occupied, walk_count, block_cols
        )
        product = jnp.einsum(
            "kiac,abkrc->kibr", operand, arrived, preferred_element_type=jnp.float32
        )
        series_term = product.reshape(local_walkers, occupied, orbitals) * (-time_root / degree)
        summed = summed + series_term
    return (summed, log_importance)


def per_device(walkers, inverse_intersection, trial, fields, cholesky):
    block_rows, block_cols, vectors = cholesky.shape
    fits = (
        block_cols == lanes
        and vectors % lanes == 0
        and 2 * walkers.shape[1] == lanes
        and block_rows % 32 == 0
        and block_rows * block_cols % (period * tile_rows) == 0
        and lax.axis_size("pair") % 2 == 0
        and lax.axis_size("walk") & (lax.axis_size("walk") - 1) == 0
    )
    step = fast if fits else plain
    return step(walkers, inverse_intersection, trial, fields, cholesky)


def solution(mesh):
    in_specs = (
        P(("walk", "pair"), None, None),
        P(("walk", "pair"), None, None),
        P(None, "walk"),
        P(("walk", "pair"), None),
        P("pair", "walk", None),
    )
    out_specs = (P(("walk", "pair"), None, None), P(("walk", "pair")))
    return jax.shard_map(
        per_device, mesh=mesh, in_specs=in_specs, out_specs=out_specs, check_vma=False
    )
```

```python
import functools

import jax
import jax.numpy as jnp
from jax import lax
from jax.experimental import pallas as pl
from jax.experimental.pallas import tpu as pltpu
from jax.sharding import PartitionSpec as P

time_root = 0.1
lanes = 128
tile_rows = 512
ring_slots = 2
ahead = 6
period = 4
early_share = 0.34

mebi = 1 << 20
grant = 13 * mebi
highest = lax.Precision.HIGHEST
whole = pl.BlockSpec(memory_space=pltpu.VMEM)
anywhere = pl.BlockSpec(memory_space=pltpu.HBM)
scalar = pl.BlockSpec(memory_space=pltpu.SMEM)


def in_vmem(array):
    return pltpu.with_memory_space_constraint(array, pltpu.VMEM)


def in_hbm(array):
    return pltpu.with_memory_space_constraint(array, pltpu.HBM)


def rotate_kernel(walkers_hbm, inverse_hbm, out_ref, walkers_ref, inverse_ref, sem):
    copies = [
        pltpu.make_async_copy(walkers_hbm, walkers_ref, sem.at[0]),
        pltpu.make_async_copy(inverse_hbm, inverse_ref, sem.at[1]),
    ]
    for copy in copies:
        copy.start()
    for copy in copies:
        copy.wait()
    count, _, orbitals = walkers_ref.shape
    half = out_ref.shape[1] // count
    pairs = orbitals // half // 2
    for w in range(count):
        turned = lax.dot_general(
            walkers_ref[w], inverse_ref[w], (((0,), (0,)), ((), ())),
            precision=highest, preferred_element_type=jnp.float32,
        )
        for b in range(pairs):
            low = turned[2 * b * half : (2 * b + 1) * half]
            high = turned[(2 * b + 1) * half : (2 * b + 2) * half]
            both = jnp.concatenate([low, high], axis=1).astype(jnp.bfloat16)
            for a in range(out_ref.shape[0] // pairs):
                out_ref[a * pairs + b, w * half : (w + 1) * half, :] = both


def rotate(walkers, inverse, walks, pairs):
    count, occupied, orbitals = walkers.shape
    half = orbitals // pairs // 2
    return pl.pallas_call(
        rotate_kernel,
        out_shape=jax.ShapeDtypeStruct(
            (walks * pairs, count * half, 2 * occupied), jnp.bfloat16
        ),
        in_specs=[anywhere, anywhere],
        out_specs=whole,
        scratch_shapes=[
            pltpu.VMEM(walkers.shape, jnp.float32),
            pltpu.VMEM(inverse.shape, jnp.float32),
            pltpu.SemaphoreType.DMA((2,)),
        ],
        compiler_params=pltpu.CompilerParams(vmem_limit_bytes=8 * mebi),
        name="rotate",
    )(in_hbm(walkers), in_hbm(inverse))


def pitch_of(rows):
    return rows + 8


def tile_access(slab_ref, kept_ref, ring, kept_sem, ring_sem):
    def view(group, i):
        if i == period - 1:
            return ring.at[group % ring_slots]
        start = (group * (period - 1) + i) * tile_rows
        return kept_ref.at[pl.ds(start, tile_rows)]

    def fetch(group, i):
        span = pl.ds((group * period + i) * tile_rows, tile_rows)
        if i == period - 1:
            sem = ring_sem.at[group % ring_slots]
        else:
            sem = kept_sem.at[group * (period - 1) + i]
        return pltpu.make_async_copy(slab_ref.at[span], view(group, i), sem)

    return fetch, view


def load_kernel(early, after_ref, slab_ref, kept_ref, sem):
    fetch, _ = tile_access(slab_ref, kept_ref, None, sem, None)
    chosen = [fetch(t // period, t % period) for t in early]
    for copy in chosen:
        copy.start()
    for copy in chosen:
        copy.wait()


def bias_kernel(count, early, core_ref, place_ref, *refs):
    parts, refs = refs[:count], refs[count:]
    trial_ref, _, slab_ref, own_ref, sent_ref, kept_ref, wide, rows, greens, total, ring, kept_sem, ring_sem = refs
    vectors = total.shape[1]
    walkers_all = total.shape[0]
    group_walkers = walkers_all // count
    half = parts[0].shape[0] // group_walkers
    occupied, columns = trial_ref.shape
    tiles = slab_ref.shape[0] // tile_rows
    blocks = vectors // lanes
    fetch, view = tile_access(slab_ref, kept_ref, ring, kept_sem, ring_sem)

    for t in range(min(ahead, tiles)):
        if t not in early:
            fetch(t // period, t % period).start()
    pitch = pitch_of(half)
    for k, part in enumerate(parts):
        top = (place_ref[0] ^ k) * (group_walkers * pitch)
        for w in range(group_walkers):
            row = pl.multiple_of(top + w * pitch, 8)
            wide[pl.ds(row, half), :] = part[w * half : (w + 1) * half, :].astype(jnp.float32)
    for r in range(half):
        rows[r * walkers_all : (r + 1) * walkers_all, :] = wide[
            pl.ds(r, walkers_all, stride=pitch), :
        ].astype(jnp.bfloat16)
    nothing = jnp.zeros((occupied, columns), jnp.bfloat16)
    trial = trial_ref[...]
    double = jnp.concatenate(
        [jnp.concatenate([trial, nothing], axis=1), jnp.concatenate([nothing, trial], axis=1)],
        axis=0,
    )
    step = 8
    for r0 in range(0, half, step):
        product = jnp.dot(
            rows[r0 * walkers_all : (r0 + step) * walkers_all, :], double,
            preferred_element_type=jnp.float32,
        ).astype(jnp.bfloat16)
        for r in range(step):
            piece = product[r * walkers_all : (r + 1) * walkers_all]
            first = (r0 + r) * columns
            second = (half + r0 + r) * columns
            greens[:, first : first + columns] = piece[:, :columns]
            greens[:, second : second + columns] = piece[:, columns:]
    for group in range(tiles // period):
        for i in range(period):
            t = group * period + i
            if t + ahead < tiles and t + ahead not in early:
                fetch((t + ahead) // period, (t + ahead) % period).start()
            if t not in early:
                fetch(group, i).wait()
            product = jnp.dot(
                greens[:, t * tile_rows : (t + 1) * tile_rows], view(group, i)[...],
                preferred_element_type=jnp.float32,
            )
            total[...] = product if t == 0 else total[...] + product

    pitch = pitch_of(walkers_all)
    for j in range(blocks):
        wide[j * pitch : j * pitch + walkers_all, :] = total[:, j * lanes : (j + 1) * lanes]
    local_walkers = own_ref.shape[1] // blocks
    core = core_ref[0]
    for g in range(own_ref.shape[0]):
        for w in range(local_walkers):
            for ref, side in ((own_ref, core), (sent_ref, 1 - core)):
                row = (2 * g + side) * local_walkers + w
                ref[g, w * blocks : (w + 1) * blocks, :] = wide[
                    pl.ds(row, blocks, stride=pitch), :
                ].astype(jnp.bfloat16)


def tiles_of(slab):
    return slab.shape[0] // tile_rows


def early_tiles(slab):
    kept = [t for t in range(tiles_of(slab)) if t % period < period - 1]
    return tuple(kept[: int(len(kept) * early_share)])


def load(after, slab):
    vectors = slab.shape[1]
    kept_tiles = tiles_of(slab) // period * (period - 1)
    early = early_tiles(slab)
    return pl.pallas_call(
        functools.partial(load_kernel, early),
        out_shape=pltpu.VMEM((kept_tiles * tile_rows, vectors), jnp.bfloat16),
        in_specs=[whole, anywhere],
        out_specs=whole,
        scratch_shapes=[pltpu.SemaphoreType.DMA((kept_tiles,))],
        compiler_params=pltpu.CompilerParams(vmem_limit_bytes=grant),
        cost_estimate=pl.CostEstimate(
            flops=0,
            bytes_accessed=2 * len(early) * tile_rows * vectors,
            transcendentals=0,
        ),
        name="load",
    )(in_vmem(after), slab)


def bias_partial(core, place, local_walkers, parts, trial, kept, slab, walkers_all):
    vectors = slab.shape[1]
    pairs = slab.shape[0]
    count = len(parts)
    half = parts[0].shape[0] * count // walkers_all
    half_shape = (
        walkers_all // local_walkers // 2, local_walkers * vectors // lanes, lanes
    )
    height = max(walkers_all * pitch_of(half), vectors // lanes * pitch_of(walkers_all))
    return pl.pallas_call(
        functools.partial(bias_kernel, count, early_tiles(slab)),
        out_shape=(
            pltpu.VMEM(half_shape, jnp.bfloat16),
            jax.ShapeDtypeStruct(half_shape, jnp.bfloat16),
            pltpu.VMEM(kept.shape, jnp.bfloat16),
        ),
        in_specs=[scalar] * 2 + [whole] * (count + 2) + [anywhere],
        out_specs=(whole, whole, whole),
        input_output_aliases={count + 3: 2},
        scratch_shapes=[
            pltpu.VMEM((height, lanes), jnp.float32),
            pltpu.VMEM((walkers_all * half, lanes), jnp.bfloat16),
            pltpu.VMEM((walkers_all, pairs), jnp.bfloat16),
            pltpu.VMEM((walkers_all, vectors), jnp.float32),
            pltpu.VMEM((ring_slots, tile_rows, vectors), jnp.bfloat16),
            pltpu.SemaphoreType.DMA((tiles_of(slab),)),
            pltpu.SemaphoreType.DMA((ring_slots,)),
        ],
        compiler_params=pltpu.CompilerParams(vmem_limit_bytes=grant),
        cost_estimate=pl.CostEstimate(
            flops=2 * walkers_all * slab.size, bytes_accessed=2 * slab.size, transcendentals=0
        ),
        name="bias_partial",
    )(core, place, *[in_vmem(part) for part in parts], trial, pltpu.with_memory_space_constraint(kept, pltpu.VMEM), slab)


def add_kernel(own_ref, other_ref, out_ref):
    added = own_ref[...].astype(jnp.float32) + other_ref[...].astype(jnp.float32)
    out_ref[...] = added.astype(jnp.bfloat16)


def add(own, other):
    return pl.pallas_call(
        add_kernel,
        out_shape=jax.ShapeDtypeStruct(own.shape, jnp.bfloat16),
        in_specs=[whole, whole],
        out_specs=whole,
        compiler_params=pltpu.CompilerParams(vmem_limit_bytes=4 * mebi),
        name="add",
    )(in_vmem(own), other)


def shift_kernel(in_ref, fields_ref, copies_ref, log_ref, turned):
    count, _, _ = in_ref.shape
    local_walkers, vectors = fields_ref.shape
    blocks = vectors // lanes
    added = in_ref[0].astype(jnp.float32)
    for s in range(1, count):
        added = added + in_ref[s].astype(jnp.float32)
    bias_shift = -time_root * added
    for j in range(blocks):
        turned[j * local_walkers : (j + 1) * local_walkers, :] = fields_ref[
            :, j * lanes : (j + 1) * lanes
        ]
    for w in range(local_walkers):
        span = slice(w * blocks, (w + 1) * blocks)
        own = turned[pl.ds(w, blocks, stride=local_walkers), :]
        shift = bias_shift[span]
        shifted = (own - shift).astype(jnp.bfloat16)
        for s in range(copies_ref.shape[0]):
            copies_ref[s, span, :] = shifted
        score = jnp.sum(own * shift - 0.5 * shift * shift, axis=0, keepdims=True)
        log_ref[w : w + 1, :] = jnp.broadcast_to(
            jnp.sum(score, axis=1, keepdims=True), (1, lanes)
        )


def shift(incoming, fields):
    count, rows, _ = incoming.shape
    local_walkers = fields.shape[0]
    return pl.pallas_call(
        shift_kernel,
        out_shape=(
            jax.ShapeDtypeStruct((count, rows, lanes), jnp.bfloat16),
            jax.ShapeDtypeStruct((local_walkers, lanes), jnp.float32),
        ),
        in_specs=[whole, whole],
        out_specs=(whole, whole),
        scratch_shapes=[pltpu.VMEM((rows, lanes), jnp.float32)],
        compiler_params=pltpu.CompilerParams(vmem_limit_bytes=4 * mebi),
        name="shift",
    )(incoming, fields)


def potential_kernel(core_ref, own_ref, other_ref, kept_ref, slab_ref, out_ref, wide, shifted, product, ring, ring_sem):
    half_rows = own_ref.shape[0]
    walkers_all, vectors = shifted.shape
    local_walkers = walkers_all // out_ref.shape[0]
    blocks = vectors // lanes
    groups = slab_ref.shape[0] // tile_rows // period
    per_tile = tile_rows // lanes
    group_rows = period * per_tile
    core = core_ref[0]
    fetch, view = tile_access(slab_ref, kept_ref, ring, None, ring_sem)

    for group in range(min(ring_slots, groups)):
        fetch(group, period - 1).start()
    pitch = pitch_of(blocks)
    for m in range(walkers_all):
        ref, row = (own_ref, m * blocks) if m * blocks < half_rows else (
            other_ref, m * blocks - half_rows
        )
        wide[m * pitch : m * pitch + blocks, :] = ref[row : row + blocks, :].astype(jnp.float32)
    for j in range(blocks):
        shifted[:, j * lanes : (j + 1) * lanes] = wide[
            pl.ds(j, walkers_all, stride=pitch), :
        ].astype(jnp.bfloat16)
    pitch = pitch_of(walkers_all)
    for group in range(groups):
        half = group % 2
        for i in range(period):
            if i == period - 1:
                fetch(group, i).wait()
            values = lax.dot_general(
                view(group, i)[...], shifted[...], (((1,), (1,)), ((), ())),
                preferred_element_type=jnp.float32,
            ).T
            for r in range(per_tile):
                row = (i * per_tile + r) * pitch
                product[half, row : row + walkers_all, :] = values[:, r * lanes : (r + 1) * lanes]
        if group + ring_slots < groups:
            fetch(group + ring_slots, period - 1).start()
        base = group * group_rows
        for m in range(walkers_all):
            side, rest = divmod(m, walkers_all // 2)
            g, w = divmod(rest, local_walkers)
            owner = 2 * g + (core if side == 0 else 1 - core)
            out_ref[owner, w, base : base + group_rows, :] = product[
                half, pl.ds(m, group_rows, stride=pitch), :
            ].astype(jnp.bfloat16)


def potential(core, local_walkers, own, other, kept, slab):
    vectors = slab.shape[1]
    walkers_all = 2 * own.shape[0] * lanes // vectors
    rows = slab.shape[0] // lanes
    return pl.pallas_call(
        potential_kernel,
        out_shape=jax.ShapeDtypeStruct(
            (walkers_all // local_walkers, local_walkers, rows, lanes), jnp.bfloat16
        ),
        in_specs=[scalar, whole, whole, whole, anywhere],
        out_specs=whole,
        scratch_shapes=[
            pltpu.VMEM((walkers_all * pitch_of(vectors // lanes), lanes), jnp.float32),
            pltpu.VMEM((walkers_all, vectors), jnp.bfloat16),
            pltpu.VMEM((2, tile_rows // lanes * period * pitch_of(walkers_all), lanes), jnp.float32),
            pltpu.VMEM((ring_slots, tile_rows, vectors), jnp.bfloat16),
            pltpu.SemaphoreType.DMA((ring_slots,)),
        ],
        compiler_params=pltpu.CompilerParams(vmem_limit_bytes=grant),
        cost_estimate=pl.CostEstimate(
            flops=2 * walkers_all * slab.size, bytes_accessed=2 * slab.size, transcendentals=0
        ),
        name="potential",
    )(core, own, other, pltpu.with_memory_space_constraint(kept, pltpu.VMEM), slab)


def series_kernel(walk_count, walkers_ref, *refs):
    pieces, out_ref, matrix = refs[:-2], refs[-2], refs[-1]
    local_walkers, _, orbitals = walkers_ref.shape
    pair_count = pieces[0].shape[0] // walk_count
    block_rows = orbitals // pair_count
    for w in range(local_walkers):
        at = 0
        for piece in pieces:
            rows = piece.shape[2]
            for a in range(walk_count):
                for b in range(pair_count):
                    top = b * block_rows + at
                    matrix[w, top : top + rows, a * lanes : (a + 1) * lanes] = piece[
                        a * pair_count + b, w
                    ]
            at += rows
    terms = [walkers_ref[w] for w in range(local_walkers)]
    sums = list(terms)
    for degree in range(1, 7):
        for w in range(local_walkers):
            terms[w] = lax.dot_general(
                terms[w].astype(jnp.bfloat16), matrix[w], (((1,), (1,)), ((), ())),
                preferred_element_type=jnp.float32,
            ) * (-time_root / degree)
            sums[w] = sums[w] + terms[w]
    for w in range(local_walkers):
        out_ref[w] = sums[w]


def series(walkers, pieces, walk_count):
    local_walkers, _, orbitals = walkers.shape
    return pl.pallas_call(
        functools.partial(series_kernel, walk_count),
        out_shape=jax.ShapeDtypeStruct(walkers.shape, jnp.float32),
        in_specs=[whole] * (1 + len(pieces)),
        out_specs=whole,
        scratch_shapes=[pltpu.VMEM((local_walkers, orbitals, orbitals), jnp.bfloat16)],
        compiler_params=pltpu.CompilerParams(vmem_limit_bytes=16 * mebi),
        name="series",
    )(walkers, *pieces)


def fast(walkers, inverse_intersection, trial, fields, cholesky):
    pair_count = lax.axis_size("pair")
    walk_count = lax.axis_size("walk")
    device_count = walk_count * pair_count
    local_walkers, occupied, _ = walkers.shape
    walkers_all = local_walkers * device_count
    vectors = cholesky.shape[2]
    slab = cholesky.reshape(-1, vectors)
    everyone = ("walk", "pair")
    exchange = functools.partial(
        lax.all_to_all, axis_name=everyone, split_axis=0, concat_axis=0, tiled=True
    )
    rotated = rotate(walkers, inverse_intersection, 1, pair_count)
    regrouped = lax.all_to_all(rotated, "pair", split_axis=0, concat_axis=0, tiled=True)
    regrouped = regrouped.reshape(-1, 2 * occupied)
    parts = [regrouped]
    for k in range(1, walk_count):
        route = [(i, i ^ k) for i in range(walk_count)]
        parts.append(lax.ppermute(regrouped, "walk", route))
    kept = load(regrouped, slab)
    core = lax.rem(lax.axis_index("pair"), 2).reshape(1)
    place = lax.axis_index("walk").reshape(1)
    swap = [(i, i ^ 1) for i in range(pair_count)]
    alike = [list(range(c, device_count, 2)) for c in range(2)]
    own, sent, kept = bias_partial(
        core, place, local_walkers, parts, trial, kept, slab, walkers_all
    )
    incoming = exchange(add(own, lax.ppermute(sent, "pair", swap)), axis_index_groups=alike)
    copies, log_rows = shift(incoming, fields)
    own = exchange(copies, axis_index_groups=alike).reshape(-1, lanes)
    other = lax.ppermute(own, "pair", swap)
    arrived = [exchange(potential(core, local_walkers, own, other, kept, slab))]
    return (series(walkers, arrived, walk_count), log_rows[:, 0])


def plain(walkers, inverse_intersection, trial, fields, cholesky):
    pair_count = lax.axis_size("pair")
    walk_count = lax.axis_size("walk")
    local_walkers, occupied, orbitals = walkers.shape
    block_rows = cholesky.shape[0]
    block_cols = cholesky.shape[1]
    vectors = cholesky.shape[2]
    flat_slab = cholesky.reshape(block_rows * block_cols, vectors)
    split_walkers = walkers.reshape(local_walkers, occupied, pair_count, block_rows)
    rotated = jnp.einsum("wji,wjbr->wbir", inverse_intersection, split_walkers, precision=highest)
    rotated = rotated.astype(jnp.bfloat16).reshape(local_walkers, pair_count, occupied * block_rows)
    regrouped = lax.all_to_all(rotated, "pair", split_axis=1, concat_axis=0, tiled=True)
    shard_piece = lax.all_gather(regrouped, "walk", axis=0, tiled=True)
    rows_here = shard_piece.shape[0]
    rotated_piece = shard_piece.reshape(rows_here, occupied, block_rows)
    greens = jnp.einsum("wir,iq->wrq", rotated_piece, trial, preferred_element_type=jnp.float32)
    greens = greens.astype(jnp.bfloat16).reshape(rows_here, block_rows * block_cols)
    partial_bias = jnp.dot(greens, flat_slab, preferred_element_type=jnp.float32)
    rows_walk = rows_here // walk_count
    outgoing = partial_bias.astype(jnp.bfloat16).reshape(walk_count, rows_walk, vectors)
    incoming = lax.all_to_all(outgoing, "walk", split_axis=0, concat_axis=0, tiled=True)
    walk_sum = jnp.sum(incoming.astype(jnp.float32), axis=0)
    outgoing = walk_sum.astype(jnp.bfloat16).reshape(pair_count, local_walkers, vectors)
    incoming = lax.all_to_all(outgoing, "pair", split_axis=0, concat_axis=0, tiled=True)
    force_bias = jnp.sum(incoming.astype(jnp.float32), axis=0)
    own_shift = -time_root * force_bias
    log_importance = jnp.sum(fields * own_shift - 0.5 * own_shift * own_shift, axis=1)
    own_shifted = (fields - own_shift).astype(jnp.bfloat16)
    pair_shifted = lax.all_gather(own_shifted, "pair", axis=0, tiled=True)
    shifted = lax.all_gather(pair_shifted, "walk", axis=0, tiled=True)
    potential = lax.dot_general(
        shifted, flat_slab, (((1,), (1,)), ((), ())), preferred_element_type=jnp.float32
    )
    potential = potential.astype(jnp.bfloat16)
    blocks = potential.reshape(walk_count * pair_count, local_walkers, block_rows, block_cols)
    arrived = lax.all_to_all(blocks, ("walk", "pair"), split_axis=0, concat_axis=0, tiled=True)
    arrived = arrived.reshape(walk_count, pair_count, local_walkers, block_rows, block_cols)
    series_term = walkers
    summed = walkers
    for degree in range(1, 7):
        operand = series_term.astype(jnp.bfloat16).reshape(
            local_walkers, occupied, walk_count, block_cols
        )
        product = jnp.einsum(
            "kiac,abkrc->kibr", operand, arrived, preferred_element_type=jnp.float32
        )
        series_term = product.reshape(local_walkers, occupied, orbitals) * (-time_root / degree)
        summed = summed + series_term
    return (summed, log_importance)


def per_device(walkers, inverse_intersection, trial, fields, cholesky):
    block_rows, block_cols, vectors = cholesky.shape
    fits = (
        block_cols == lanes
        and vectors % lanes == 0
        and 2 * walkers.shape[1] == lanes
        and block_rows % 32 == 0
        and block_rows * block_cols % (period * tile_rows) == 0
        and lax.axis_size("pair") % 2 == 0
        and lax.axis_size("walk") & (lax.axis_size("walk") - 1) == 0
    )
    step = fast if fits else plain
    return step(walkers, inverse_intersection, trial, fields, cholesky)


def solution(mesh):
    in_specs = (
        P(("walk", "pair"), None, None),
        P(("walk", "pair"), None, None),
        P(None, "walk"),
        P(("walk", "pair"), None),
        P("pair", "walk", None),
    )
    out_specs = (P(("walk", "pair"), None, None), P(("walk", "pair")))
    return jax.shard_map(
        per_device, mesh=mesh, in_specs=in_specs, out_specs=out_specs, check_vma=False
    )
```
